32 devices in a mesh: group: 2 (over y), lon: 16 (over z, x, core).
Axes of the slice: x: 2, y: 2, z: 4, core: 2. Of those that a mesh axis runs over, the one named last changes fastest.
Arguments:
- tokens: bfloat16 [128, 32, 64, 128], P('group', 'lon'), parts along dimension 0, may hold values from -600 to 600, as said below
- neighbours: int32 [64, 32, 9], P(None, 'lon'), may hold values from 0 to 2047, as said below
- time_step: int32 [2], P('group'), parts along dimension 0, may hold values from 0 to 999
- time_weight: bfloat16 [256, 128], replicated, may hold values from -0.375 to 0.375
- fine_project: bfloat16 [128, 384], replicated, may hold values from -0.5 to 0.5
- fine_output: bfloat16 [128, 128], replicated, may hold values from -0.5 to 0.5
- fine_scale: float32 [2], replicated, may hold values from 8 to 400
- coarse_input: bfloat16 [128, 1024], replicated, may hold values from -0.5 to 0.5
- coarse_project: bfloat16 [1024, 3072], replicated, may hold values from -0.1875 to 0.1875
- coarse_scale: float32 [16], replicated, may hold values from 8 to 400
- coarse_output: bfloat16 [1024, 128], replicated, may hold values from -0.1875 to 0.1875
Outputs:
- update: bfloat16 [128, 32, 64, 128], P('group', 'lon'), parts along dimension 0
The draws below stay inside these ranges and needn't reach their ends.
There are 2 independent parts, one for each index of `group`. The reference program is written for one: setup_inputs(seed, part) draws one part's arguments, and reference() takes and returns one part's arrays. A program takes and returns all parts, laid end to end along the dimension named above; an argument that names none is the same for every part. Nothing has to cross between parts.
Inputs may be any that keep to these rules, and one draw needn't show every extreme that they name: `tokens`: values carry scales that differ from token to token and from feature to feature. `neighbours`: entry s of a tile's list names a tile whose longitude column is the tile's plus s // 3 - 1, cyclically over 32 columns, and whose latitude row lies within one of the tile's, clamped to 0 .. 63; entry 4 is the tile itself.
All inputs are finite; a program needn't handle non-finite values.
Results may differ from the reference program's by a relative error of at most 0.025.
Values may be sent and summed in bfloat16 or wider, within the bound.
No kernel may reach another device: no remote copies, remote signals or barrier semaphores. Data moves between devices by JAX's collectives and lax.ppermute only.
A program may use at most 128 MiB of HBM per device.

```python
import math
import jax
import jax.numpy as jnp
from jax import lax

D = 128
DC = 1024
HD = 64
DE = 256
TILE = 8
POOL = 32
TLAT = 64
NTLON = 32


def draw_tokens(key, part):
    base_key, row_key, column_key = jax.random.split(key, 3)
    shape = (TLAT, NTLON, TILE * TILE, D)
    row_scale = jnp.exp(jax.random.uniform(row_key, (TLAT, NTLON, TILE * TILE, 1), jnp.float32, 0.0, math.log(10.0)))
    column_scale = jnp.exp(jax.random.uniform(column_key, (D,), jnp.float32, 0.0, math.log(10.0)))
    base = jnp.clip(jax.random.normal(base_key, shape, jnp.float32), -6.0, 6.0)
    return (base * row_scale * column_scale).astype(jnp.bfloat16)


def scale_draw(key, heads):
    highest = 32.0
    return jnp.exp(jax.random.uniform(key, (heads,), jnp.float32, math.log(8.0), math.log(highest)))


def draw_fine_scale(key, part):
    return scale_draw(jax.random.fold_in(key, 11), D // HD)


def draw_coarse_scale(key, part):
    return scale_draw(jax.random.fold_in(key, 23), DC // HD)


def draw_neighbours(key, part):
    slots = jnp.arange(9, dtype=jnp.int32)
    row_steps = jax.random.randint(jax.random.fold_in(key, 5), (TLAT, NTLON, 9), -1, 2, jnp.int32)
    row_steps = jnp.where(slots == 4, 0, row_steps)
    column_steps = slots // 3 - 1
    rows = jnp.clip(jnp.arange(TLAT, dtype=jnp.int32)[:, None, None] + row_steps, 0, TLAT - 1)
    columns = (jnp.arange(NTLON, dtype=jnp.int32)[None, :, None] + column_steps + NTLON) % NTLON
    return (rows * NTLON + columns).astype(jnp.int32)


def bell_draw(rng, extent, spread, most, kind=jnp.bfloat16):
    return jnp.clip(spread * jax.random.normal(rng, extent, jnp.float32), -most, most).astype(kind)


def setup_inputs(seed: int = 0, part: int = 0) -> dict:
    key_of = jax.random.split(jax.random.key(seed), 12)
    part_keys = jax.random.split(jax.random.fold_in(key_of[11], part), 12)
    return {
        "tokens": draw_tokens(jax.random.fold_in(jax.random.fold_in(key_of[11], part), 71), part),
        "neighbours": draw_neighbours(jax.random.fold_in(key_of[11], 71), part),
        "time_step": jax.random.randint(part_keys[2], (1,), 0, 1000).astype(jnp.int32),
        "time_weight": bell_draw(key_of[3], (DE, D), DE ** -0.5, 0.375),
        "fine_project": bell_draw(key_of[4], (D, 3 * D), D ** -0.5, 0.5),
        "fine_output": bell_draw(key_of[5], (D, D), D ** -0.5, 0.5),
        "fine_scale": draw_fine_scale(jax.random.fold_in(key_of[11], 71), part),
        "coarse_input": bell_draw(key_of[7], (D, DC), D ** -0.5, 0.5),
        "coarse_project": bell_draw(key_of[8], (DC, 3 * DC), DC ** -0.5, 0.1875),
        "coarse_scale": draw_coarse_scale(jax.random.fold_in(key_of[11], 71), part),
        "coarse_output": bell_draw(key_of[10], (DC, D), DC ** -0.5, 0.1875),
    }


EPS = 1e-06

def time_features(time_step, size):
    half = size // 2
    freqs = jnp.exp(jnp.arange(half, dtype=jnp.float32) * (-math.log(10000.0) / half))
    angles = time_step.astype(jnp.float32)[0] * freqs
    return jnp.concatenate([jnp.cos(angles), jnp.sin(angles)])

def head_normal(values, head_size):
    shaped = values.reshape(values.shape[:-1] + (values.shape[-1] // head_size, head_size))
    scaled = shaped * lax.rsqrt(lax.optimization_barrier(jnp.sum(shaped * shaped, axis=-1, keepdims=True)) + EPS)
    return scaled.reshape(values.shape)

def modulate(tokens, modulation):
    values = tokens.astype(jnp.float32)
    factor = lax.rsqrt(lax.optimization_barrier(jnp.mean(values * values, axis=-1, keepdims=True)) + EPS)
    return (values * factor * (1.0 + modulation)).astype(jnp.bfloat16)

def attend(query, keys, values, head_size):
    count, rows, width = query.shape
    heads = width // head_size
    length = keys.shape[1]
    query_heads = lax.optimization_barrier(query).astype(jnp.float32).reshape(count, rows, heads, head_size)
    key_heads = lax.optimization_barrier(keys).astype(jnp.float32).reshape(count, length, heads, head_size)
    value_heads = lax.optimization_barrier(values).astype(jnp.float32).reshape(count, length, heads, head_size)
    scores = jnp.einsum('tqhd,tkhd->thqk', query_heads, key_heads)
    largest = lax.optimization_barrier(jnp.max(scores, axis=-1, keepdims=True))
    raised = jnp.exp(scores - largest)
    totals = lax.optimization_barrier(jnp.sum(raised, axis=-1))
    weights = lax.optimization_barrier(raised.astype(jnp.bfloat16)).astype(jnp.float32)
    mixed = jnp.einsum('thqk,tkhd->tqhd', weights, value_heads)
    mixed = mixed / jnp.transpose(totals, (0, 2, 1))[..., None]
    return mixed.reshape(count, rows, width).astype(jnp.bfloat16)

def reference(tokens, neighbours, time_step, time_weight, fine_project, fine_output, fine_scale, coarse_input, coarse_project, coarse_scale, coarse_output):
    features = time_features(time_step, DE)
    modulation = jnp.dot(features.astype(jnp.bfloat16)[None, :], time_weight, preferred_element_type=jnp.float32)[0]
    normed = modulate(tokens, modulation)
    cells = TILE * TILE
    fine_scales = jnp.repeat(fine_scale, HD)

    def fine_row(row):
        projected = jnp.dot(row.reshape(-1, D), fine_project, preferred_element_type=jnp.float32)
        query = (head_normal(projected[:, :D], HD) * fine_scales).astype(jnp.bfloat16)
        keys = head_normal(projected[:, D:2 * D], HD).astype(jnp.bfloat16)
        values = projected[:, 2 * D:].astype(jnp.bfloat16)
        paired = jnp.concatenate([keys, values], axis=-1)
        return (query.reshape(NTLON, cells, D), paired.reshape(NTLON, cells, 2 * D))
    queries, key_values = lax.map(fine_row, normed)
    flat_pairs = key_values.reshape(TLAT * NTLON, cells, 2 * D)

    def fine_attend(block):
        query_row, lists = block
        gathered = flat_pairs[lists].reshape(NTLON, 9 * cells, 2 * D)
        mixed = attend(query_row, gathered[..., :D], gathered[..., D:], HD)
        return jnp.dot(mixed.reshape(-1, D), fine_output, preferred_element_type=jnp.float32).reshape(NTLON, cells, D)
    fine_update = lax.map(fine_attend, (queries, neighbours))
    side = POOL // TILE
    cell_rows = TLAT // side
    cell_cols = NTLON // side
    grouped = normed.reshape(cell_rows, side, cell_cols, side, cells, D)
    pooled = (lax.optimization_barrier(jnp.sum(grouped, axis=(1, 3, 4), dtype=jnp.float32)) / (POOL * POOL)).astype(jnp.bfloat16)
    raw = jnp.dot(pooled.reshape(-1, D), coarse_input, preferred_element_type=jnp.float32)
    coarse = (raw * lax.rsqrt(lax.optimization_barrier(jnp.mean(raw * raw, axis=-1, keepdims=True)) + EPS)).astype(jnp.bfloat16)
    coarse_projected = jnp.dot(coarse, coarse_project, preferred_element_type=jnp.float32)
    coarse_query = (head_normal(coarse_projected[:, :DC], HD) * jnp.repeat(coarse_scale, HD)).astype(jnp.bfloat16)
    coarse_keys = head_normal(coarse_projected[:, DC:2 * DC], HD).astype(jnp.bfloat16)
    coarse_values = coarse_projected[:, 2 * DC:].astype(jnp.bfloat16)
    coarse_mixed = attend(coarse_query[None], coarse_keys[None], coarse_values[None], HD)[0]
    coarse_update = jnp.dot(coarse_mixed, coarse_output, preferred_element_type=jnp.float32).reshape(cell_rows, cell_cols, D)
    update = fine_update.reshape(cell_rows, side, cell_cols, side, cells, D) + coarse_update[:, None, :, None, None, :]
    return update.reshape(TLAT, NTLON, cells, D).astype(jnp.bfloat16)
```

```python
import math, functools
import numpy as np
import jax, jax.numpy as jnp
from jax import lax
from jax.sharding import PartitionSpec as P
from jax.experimental import pallas as pl
from jax.experimental.pallas import tpu as pltpu

EPS = 1e-6
LOG2E = math.log2(math.e)
HD = 64
TILE = 8
POOL = 32
bf16, f32 = jnp.bfloat16, jnp.float32
NT = (((1,), (1,)), ((), ()))
NN = (((1,), (0,)), ((), ()))

def dot(a, b, dims=NN):
    return lax.dot_general(a, b, dims, preferred_element_type=f32)

def block_sum(values, ones):
    high = values.astype(bf16)
    low = (values - high.astype(f32)).astype(bf16)
    return dot(jnp.concatenate([high, low], axis=1), ones)

def normed_of(x, gain, ones):
    v = x.astype(f32)
    mean = jnp.mean(v * v, axis=-1, keepdims=True)
    return (v * lax.rsqrt(mean + EPS) * gain).astype(bf16)

def ones_block(width, size):
    blocks = np.kron(np.eye(width // size), np.ones((size, size)))
    return np.concatenate([blocks, blocks], axis=0)

def project_kernel(with_query, rows, tok_ref, gain_ref, wqk_ref, wvt_ref, ones_ref, scale_ref, *outs):
    i = pl.program_id(1)
    if with_query:
        q_ref, k_ref, vt_ref = outs
    else:
        k_ref, vt_ref = outs
    cells = tok_ref.shape[-2]
    width = tok_ref.shape[-1]
    n = rows * cells
    x = tok_ref[...].reshape(n, width)
    normed = normed_of(x, gain_ref[...], None)
    ones = ones_ref[...]
    qk = dot(normed, wqk_ref[...])
    if with_query:
        q = qk[:, :width]
        q = q * lax.rsqrt(block_sum(q * q, ones) + EPS) * scale_ref[...]
        q_ref[0] = q.astype(bf16)
        k = qk[:, width:]
    else:
        k = qk
    k = k * lax.rsqrt(block_sum(k * k, ones) + EPS)
    k_ref[0] = k.astype(bf16)
    vt_ref[0] = dot(wvt_ref[...], normed, NT).astype(bf16)

def project(tokens, gain, wqk, wvt, ones, scale, with_query, rows=8):
    lat, columns, cells, width = tokens.shape
    n = rows * cells
    const = lambda a: pl.BlockSpec(a.shape, lambda c, i: (0,) * a.ndim)
    tshape = jax.ShapeDtypeStruct((columns, lat * cells, width), bf16)
    vshape = jax.ShapeDtypeStruct((columns, width, lat * cells), bf16)
    tspec = pl.BlockSpec((1, n, width), lambda c, i: (c, i, 0))
    vspec = pl.BlockSpec((1, width, n), lambda c, i: (c, 0, i))
    outs = [tshape, vshape]; specs = [tspec, vspec]
    if with_query:
        outs = [tshape] + outs; specs = [tspec] + specs
    return pl.pallas_call(
        functools.partial(project_kernel, with_query, rows),
        grid=(columns, lat // rows),
        in_specs=[pl.BlockSpec((rows, 1, cells, width), lambda c, i: (i, c, 0, 0)),
                  const(gain), const(wqk), const(wvt), const(ones), const(scale)],
        out_specs=specs, out_shape=outs, name="project",
    )(tokens, gain, wqk, wvt, ones, scale)

def attend_kernel(rows, ncol, lw_ref, *refs):
    q_refs = refs[:ncol]
    k_refs = refs[ncol:2 * ncol + 2]
    v_refs = refs[2 * ncol + 2:3 * ncol + 4]
    wo_ref, cu_ref, out_ref, p_ref = refs[3 * ncol + 4:]
    i = pl.program_id(0)
    cells = HD
    width = wo_ref.shape[0]

    @pl.when(i == 0)
    def _():
        p_ref[...] = jnp.zeros_like(p_ref)

    lane = lax.broadcasted_iota(jnp.int32, (cells, width), 1)
    first = lane < HD
    wo = wo_ref[...]

    def pair_rows(p, carry):
        off = pl.multiple_of(p * 2 * cells, 2 * cells)
        for c in range(ncol):
            q2 = q_refs[c][0, pl.ds(off, 2 * cells), :]
            zero = jnp.zeros((cells, width), bf16)
            qbd = jnp.concatenate(
                [jnp.where(first, q2[:cells], zero), jnp.where(first, zero, q2[:cells]),
                 jnp.where(first, q2[cells:], zero), jnp.where(first, zero, q2[cells:])], axis=0)
            row = i * rows + p * 2
            base = [((row + t) * ncol + c) * 9 for t in range(2)]
            s = []
            for j in range(3):
                kj = k_refs[c + j][0, pl.ds(off, 4 * cells), :]
                s.append(dot(kj, qbd, NT))
            tots = []
            for t in range(2):
                ls = slice(t * width, (t + 1) * width)
                m = None
                lws = {}
                for j in range(3):
                    for u in range(3):
                        lw = lw_ref[base[t] + j * 3 + u]
                        lws[j, u] = lw
                        blk = s[j][(t + u) * cells:(t + u + 1) * cells, ls]
                        pm = jnp.max(blk.reshape(cells // 8, 8, width), axis=0) + jnp.minimum(lw, 0.0)
                        m = pm if m is None else jnp.maximum(m, pm)
                m = jnp.max(m, axis=0, keepdims=True) * LOG2E
                tot = None
                for j in range(3):
                    for u in range(3):
                        blk = s[j][(t + u) * cells:(t + u + 1) * cells, ls]
                        e = jnp.exp2(blk * LOG2E - (m - lws[j, u]))
                        ps = jnp.sum(e.reshape(cells // 8, 8, width), axis=0)
                        tot = ps if tot is None else tot + ps
                        p_ref[c, j, (t + u) * cells:(t + u + 1) * cells, ls] = e.astype(bf16)
                tots.append(1.0 / jnp.sum(tot, axis=0, keepdims=True))
            o = None
            for j in range(3):
                vj = v_refs[c + j][0, :, pl.ds(off, 4 * cells)]
                d = dot(vj, p_ref[c, j])
                o = d if o is None else o + d
            mixed = []
            for t in range(2):
                ot = (o[:, t * width:(t + 1) * width] * tots[t]).T
                mixed.append(jnp.where(first, ot[:cells], ot[cells:]).astype(bf16))
            up = dot(jnp.concatenate(mixed, axis=0), wo)
            cu = cu_ref[pl.ds(row // 4, 1), :]
            out_ref[pl.ds(p * 2, 2), c] = (up + cu).astype(bf16).reshape(2, cells, width)
        return carry
    lax.fori_loop(0, rows // 2, pair_rows, 0)

def attend(lw, qs, ks, vs, wo, cu, lat, rows=8, unroll=1):
    ncol = len(qs)
    cells = HD
    width = wo.shape[0]
    n = rows * cells
    qspec = pl.BlockSpec((1, n, width), lambda i: (0, i, 0))
    kspec = pl.BlockSpec((pl.Element(1), pl.Element(n + 2 * cells), pl.Element(width)), lambda i: (0, i * n, 0))
    vspec = pl.BlockSpec((pl.Element(1), pl.Element(width), pl.Element(n + 2 * cells)), lambda i: (0, 0, i * n))
    return pl.pallas_call(
        functools.partial(attend_kernel, rows, ncol),
        grid=(lat // rows,),
        in_specs=[pl.BlockSpec(memory_space=pltpu.SMEM)] + [qspec] * ncol + [kspec] * (ncol + 2) + [vspec] * (ncol + 2)
        + [pl.BlockSpec(wo.shape, lambda i: (0, 0)), pl.BlockSpec(cu.shape, lambda i: (0, 0))],
        out_specs=pl.BlockSpec((rows, ncol, cells, width), lambda i: (i, 0, 0, 0)),
        out_shape=jax.ShapeDtypeStruct((lat, ncol, cells, width), bf16),
        scratch_shapes=[pltpu.VMEM((ncol, 3, 4 * cells, 2 * width), bf16)],
        name="attend",
    )(lw, *qs, *ks, *vs, wo, cu)


def pool_kernel(side, step_ref, freq_ref, weight_ref, tok_ref, part_ref, gain_ref):
    i = pl.program_id(0)
    rows, columns, cells, width = tok_ref.shape

    @pl.when(i == 0)
    def _():
        angles = step_ref[0].astype(f32) * freq_ref[...]
        features = jnp.concatenate([jnp.cos(angles), jnp.sin(angles)], axis=1).astype(bf16)
        gain_ref[...] = 1.0 + dot(features, weight_ref[...])

    gain = gain_ref[...][:1]
    for g in range(rows // side):
        x = tok_ref[g * side:(g + 1) * side].reshape(side * columns * cells, width)
        normed = normed_of(x, gain, None).astype(f32)
        total = jnp.sum(normed.reshape(-1, 8, width), axis=0)
        part_ref[pl.ds(i * (rows // side) + g, 1), :] = jnp.sum(total, axis=0, keepdims=True)

def pool(tokens, time_step, freqs, time_weight, rows=16):
    lat, columns, cells, width = tokens.shape
    side = POOL // TILE
    return pl.pallas_call(
        functools.partial(pool_kernel, side),
        grid=(lat // rows,),
        in_specs=[pl.BlockSpec(memory_space=pltpu.SMEM),
                  pl.BlockSpec(freqs.shape, lambda i: (0, 0)),
                  pl.BlockSpec(time_weight.shape, lambda i: (0, 0)),
                  pl.BlockSpec((rows, columns, cells, width), lambda i: (i, 0, 0, 0))],
        out_specs=[pl.BlockSpec((lat // side, width), lambda i: (0, 0)), pl.BlockSpec((8, width), lambda i: (0, 0))],
        out_shape=[jax.ShapeDtypeStruct((lat // side, width), f32), jax.ShapeDtypeStruct((8, width), f32)],
        name="pool",
    )(time_step, freqs, time_weight, tokens)

def coarse_kernel(pair, nblocks, *refs):
    blocks = refs[:nblocks]
    cin_ref, wq_ref, wk_ref, wv_ref, wo_ref, scale_ref, ones_ref, out_ref, coarse_ref = refs[nblocks:]
    g = pl.program_id(0)
    cell_rows, width = out_ref.shape

    @pl.when(g == 0)
    def _():
        parts = []
        for ref in blocks:
            value = ref[...]
            parts += [value[a * cell_rows:(a + 1) * cell_rows] for a in range(value.shape[0] // cell_rows)]
        pooled = []
        for a in range(0, len(parts), pair):
            total = parts[a]
            for b in range(1, pair):
                total = total + parts[a + b]
            pooled.append(total)
        pooled = (jnp.concatenate(pooled, axis=0) / (POOL * POOL)).astype(bf16)
        raw = dot(pooled, cin_ref[...])
        coarse_ref[...] = (raw * lax.rsqrt(jnp.mean(raw * raw, axis=-1, keepdims=True) + EPS)).astype(bf16)
        out_ref[...] = jnp.zeros_like(out_ref)

    coarse = coarse_ref[...]
    sub = wq_ref.shape[1]
    heads = sub // HD
    ones = ones_ref[...]
    lane_head = lax.broadcasted_iota(jnp.int32, (cell_rows, sub), 1) // HD
    q = dot(coarse[:cell_rows], wq_ref[...])
    q = (q * lax.rsqrt(block_sum(q * q, ones) + EPS) * scale_ref[...]).astype(bf16)
    k = dot(coarse, wk_ref[...])
    k = (k * lax.rsqrt(block_sum(k * k, ones) + EPS)).astype(bf16)
    v = dot(coarse, wv_ref[...]).astype(bf16)
    qbd = jnp.concatenate([jnp.where(lane_head == h, q, jnp.zeros_like(q)) for h in range(heads)], axis=0)
    s = dot(qbd, k, NT)
    e = jnp.exp(s - jnp.max(s, axis=-1, keepdims=True))
    o = dot(e.astype(bf16), v) / jnp.sum(e, axis=-1, keepdims=True)
    mixed = o[:cell_rows]
    for h in range(1, heads):
        mixed = jnp.where(lane_head == h, o[h * cell_rows:(h + 1) * cell_rows], mixed)
    out_ref[...] += dot(mixed.astype(bf16), wo_ref[...])

def coarse_level(blocks, coarse_input, coarse_project, coarse_scale, coarse_output, cell_rows, pair, sub=256):
    width, dc = coarse_input.shape
    steps = dc // sub
    ncells = sum(b.shape[0] for b in blocks) // pair
    ones = jnp.asarray(ones_block(sub, HD), bf16)
    scale = jnp.repeat(coarse_scale, HD)[None, :]
    whole = lambda a: pl.BlockSpec(a.shape, lambda g: (0,) * a.ndim)
    return pl.pallas_call(
        functools.partial(coarse_kernel, pair, len(blocks)),
        grid=(steps,),
        in_specs=[whole(b) for b in blocks] + [
            whole(coarse_input),
            pl.BlockSpec((dc, sub), lambda g: (0, g)),
            pl.BlockSpec((dc, sub), lambda g: (0, steps + g)),
            pl.BlockSpec((dc, sub), lambda g: (0, 2 * steps + g)),
            pl.BlockSpec((sub, width), lambda g: (g, 0)),
            pl.BlockSpec((1, sub), lambda g: (0, g)),
            whole(ones)],
        out_specs=pl.BlockSpec((cell_rows, width), lambda g: (0, 0)),
        out_shape=jax.ShapeDtypeStruct((cell_rows, width), f32),
        scratch_shapes=[pltpu.VMEM((ncells, dc), bf16)],
        name="coarse",
    )(*blocks, coarse_input, coarse_project, coarse_project, coarse_project, coarse_output, scale, ones)

def gather_stages(size, radix=4):
    stages, stride = [], 1
    while stride < size:
        count = min(radix, size // stride)
        stages.append((stride, count))
        stride *= count
    return stages

def gather_blocks(value, axis):
    size = lax.axis_size(axis)
    blocks = [value]
    for stride, count in gather_stages(size):
        held = blocks[0] if len(blocks) == 1 else jnp.concatenate(blocks, axis=0)
        blocks = [held] if len(blocks) == 1 else blocks
        for other in range(1, count):
            pairs = [(source, source ^ (other * stride)) for source in range(size)]
            blocks = blocks + [lax.ppermute(held, axis, pairs)]
    return blocks

def shards(tokens, neighbours, time_step, time_weight, fine_project, fine_output, fine_scale,
           coarse_input, coarse_project, coarse_scale, coarse_output):
    lat, columns, cells, width = tokens.shape
    size = lax.axis_size("lon")
    up = [(i, (i + 1) % size) for i in range(size)]
    down = [(j, i) for i, j in up]
    before = lax.ppermute(tokens[:, columns - 1:], "lon", up)
    after = lax.ppermute(tokens[:, :1], "lon", down)

    half = time_weight.shape[0] // 2
    freqs = jnp.asarray(np.exp(np.arange(half) * (-math.log(10000.0) / half))[None, :].repeat(8, 0), f32)
    part, gain8 = pool(tokens, time_step, freqs, time_weight)
    gain = gain8[:1]
    blocks = gather_blocks(part, "lon")

    step = neighbours // (columns * size) - jnp.arange(lat, dtype=jnp.int32)[:, None, None]
    near = step.reshape(lat, columns, 3, 1, 3) == jnp.arange(-1, 2, dtype=jnp.int32)[:, None]
    count = jnp.sum(near.astype(jnp.int32), axis=-1)
    log_count = jnp.where(count == 0, -1e30, jnp.where(count == 1, 0.0, jnp.where(count == 2, 1.0, math.log2(3.0))))
    lw = log_count.astype(f32).reshape(-1)

    ones = jnp.asarray(ones_block(width, HD), bf16)
    scale = jnp.repeat(fine_scale, HD)[None, :]
    wqk = fine_project[:, :2 * width]
    wvt = fine_project[:, 2 * width:].T
    q, k, vt = project(tokens, gain, wqk, wvt, ones, scale, True, rows=16)
    sides = [project(x, gain, wqk[:, width:], wvt, ones, scale, False, rows=16) for x in (before, after)]
    pad_k = lambda a: jnp.pad(a, ((0, 0), (cells, cells), (0, 0)))
    pad_v = lambda a: jnp.pad(a, ((0, 0), (0, 0), (cells, cells)))
    ks = [sides[0][0]] + [k[c:c + 1] for c in range(columns)] + [sides[1][0]]
    vs = [sides[0][1]] + [vt[c:c + 1] for c in range(columns)] + [sides[1][1]]
    side = POOL // TILE
    pair = POOL // (TILE * columns)
    cu = coarse_level(blocks, coarse_input, coarse_project, coarse_scale, coarse_output, lat // side, pair)
    return attend(lw, [q[c:c + 1] for c in range(columns)], [pad_k(a) for a in ks], [pad_v(a) for a in vs],
                  fine_output, cu, lat, rows=16)

def solution(mesh):
    return jax.shard_map(
        shards,
        mesh=mesh,
        in_specs=(P("group", "lon", None, None), P(None, "lon", None), P("group"),
                  P(), P(), P(), P(), P(), P(), P(), P()),
        out_specs=P("group", "lon", None, None),
        check_vma=False,
    )
```

```python
import functools
import math

import jax
import jax.numpy as jnp
import numpy as np
from jax import lax
from jax.experimental import pallas as pl
from jax.experimental.pallas import tpu as pltpu
from jax.sharding import PartitionSpec as P

HD = 64
TILE = 8
POOL = 32
EPS = 1e-6
LOG2E = math.log2(math.e)
SIDE = POOL // TILE
bf16, f32 = jnp.bfloat16, jnp.float32
NT = (((1,), (1,)), ((), ()))
NN = (((1,), (0,)), ((), ()))
SMEM = pl.BlockSpec(memory_space=pltpu.SMEM)
ANY = pl.BlockSpec(memory_space=pl.ANY)


def dot(a, b, dims=NN):
    return lax.dot_general(a, b, dims, preferred_element_type=f32)


def whole(a):
    return pl.BlockSpec(a.shape, lambda i: (0,) * a.ndim)


def ones_block(width, size):
    blocks = np.kron(np.eye(width // size), np.ones((size, size)))
    return jnp.asarray(np.concatenate([blocks, blocks], axis=0), bf16)


def block_sum(values, ones):
    high = values.astype(bf16)
    low = (values - high.astype(f32)).astype(bf16)
    return dot(jnp.concatenate([high, low], axis=1), ones)


def head_scales(scale_ref, start, width):
    head = lax.broadcasted_iota(jnp.int32, (1, width), 1) // HD
    out = jnp.zeros((1, width), f32)
    for h in range(width // HD):
        out = jnp.where(head == h, scale_ref[start + h], out)
    return out


def normed_of(x, gain):
    v = x.astype(f32)
    mean = jnp.mean(v * v, axis=-1, keepdims=True)
    return (v * lax.rsqrt(mean + EPS) * gain).astype(bf16)


def edges_kernel(tok_ref, first_ref, last_ref, sem):
    columns = tok_ref.shape[1]
    copies = [
        pltpu.make_async_copy(tok_ref.at[:, pl.ds(columns - 1, 1)], last_ref, sem.at[0]),
        pltpu.make_async_copy(tok_ref.at[:, pl.ds(0, 1)], first_ref, sem.at[1]),
    ]
    for copy in copies:
        copy.start()
    for copy in copies:
        copy.wait()


def edges(tokens):
    lat, _, cells, width = tokens.shape
    shape = jax.ShapeDtypeStruct((lat, 1, cells, width), tokens.dtype)
    return pl.pallas_call(
        edges_kernel,
        in_specs=[ANY],
        out_specs=[ANY, ANY],
        out_shape=[shape, shape],
        scratch_shapes=[pltpu.SemaphoreType.DMA((2,))],
        name="edges",
    )(tokens)


def pool_kernel(step_ref, freq_ref, weight_ref, tok_ref, part_ref, gain_ref):
    i = pl.program_id(0)
    rows, columns, cells, width = tok_ref.shape

    @pl.when(i == 0)
    def _():
        angles = step_ref[0].astype(f32) * freq_ref[...]
        features = jnp.concatenate([jnp.cos(angles), jnp.sin(angles)], axis=1).astype(bf16)
        gain_ref[...] = 1.0 + dot(features, weight_ref[...])

    gain = gain_ref[:1, :]
    for g in range(rows // SIDE):
        x = tok_ref[g * SIDE:(g + 1) * SIDE].reshape(SIDE * columns * cells, width)
        normed = normed_of(x, gain).astype(f32)
        total = jnp.sum(normed.reshape(-1, 8, width), axis=0)
        part_ref[pl.ds(i * (rows // SIDE) + g, 1), :] = jnp.sum(total, axis=0, keepdims=True)


def pool(tokens, time_step, time_weight, rows=16):
    lat, columns, cells, width = tokens.shape
    half = time_weight.shape[0] // 2
    freqs = np.exp(np.arange(half) * (-math.log(10000.0) / half))
    freqs = jnp.asarray(np.tile(freqs[None, :], (8, 1)), f32)
    shapes = [jax.ShapeDtypeStruct((lat // SIDE, width), f32), jax.ShapeDtypeStruct((8, width), f32)]
    return pl.pallas_call(
        pool_kernel,
        grid=(lat // rows,),
        in_specs=[SMEM, whole(freqs), whole(time_weight),
                  pl.BlockSpec((rows, columns, cells, width), lambda i: (i, 0, 0, 0))],
        out_specs=[whole(s) for s in shapes],
        out_shape=shapes,
        name="pool",
    )(time_step, freqs, time_weight, tokens)


def join_kernel(run, *refs):
    blocks, out_ref = refs[:-1], refs[-1]
    size = blocks[0].shape[0]
    for a in range(0, len(blocks), run):
        total = blocks[a][...]
        for b in range(1, run):
            total = total + blocks[a + b][...]
        out_ref[a // run * size:(a // run + 1) * size, :] = total


def join(blocks, run):
    size, width = blocks[0].shape
    shape = jax.ShapeDtypeStruct((len(blocks) // run * size, width), f32)
    return pl.pallas_call(functools.partial(join_kernel, run), out_shape=shape, name="join")(*blocks)


def gather_cells(part, axis, run):
    size = lax.axis_size(axis)
    held, blocks, stride = part, [part], 1
    while stride < size:
        count = min(4, size // stride)
        blocks = [held]
        for other in range(1, count):
            pairs = [(source, source ^ (other * stride)) for source in range(size)]
            blocks.append(lax.ppermute(held, axis, pairs))
        stride *= count
        if stride < size or run > 1:
            held = join(blocks, run)
            blocks, run = [held], 1
    return blocks


def project_kernel(with_query, rows, scale_ref, tok_ref, gain_ref, w_ref, ones_ref, *refs):
    outs, carry_ref = refs[:-1], refs[-1]
    k_ref, v_ref = outs[-2:]
    lat, _, cells, width = tok_ref.shape
    n = rows * cells
    ones = ones_ref[...]
    gain = gain_ref[:1, :]
    w = w_ref[...] if with_query else w_ref[:, width:]
    base = w.shape[1] - 2 * width
    zero = jnp.zeros((cells, width), bf16)
    k_ref[:cells, :] = zero
    k_ref[(lat + 1) * cells:, :] = zero
    carry_ref[...] = jnp.zeros_like(carry_ref)
    if with_query:
        scale = head_scales(scale_ref, 0, width)

    def chunk(i, carry):
        normed = normed_of(tok_ref[pl.ds(i * rows, rows), 0].reshape(n, width), gain)
        off = pl.multiple_of(i * n, n)
        out = dot(normed, w)
        if with_query:
            q = out[:, :width]
            outs[0][pl.ds(off, n), :] = (q * lax.rsqrt(block_sum(q * q, ones) + EPS) * scale).astype(bf16)
        k = out[:, base:base + width]
        k = k * lax.rsqrt(block_sum(k * k, ones) + EPS)
        k_ref[pl.ds(pl.multiple_of(off + cells, cells), n), :] = k.astype(bf16)
        v = jnp.concatenate([carry_ref[...], out[:, base + width:]], axis=0)
        for b in range(rows // 2):
            v_ref[i * (rows // 2) + b] = v[b * 2 * cells:(b + 1) * 2 * cells].T.astype(bf16)
        carry_ref[...] = v[n:]
        return carry

    lax.fori_loop(0, lat // rows, chunk, 0)
    last = jnp.concatenate([carry_ref[...], jnp.zeros_like(carry_ref)], axis=0)
    v_ref[lat // 2] = last.T.astype(bf16)


def project(tokens, column, gain, weights, ones, scale, with_query, rows=16):
    lat, _, cells, width = tokens.shape
    shapes = [jax.ShapeDtypeStruct(((lat + 2) * cells, width), bf16),
              jax.ShapeDtypeStruct((lat // 2 + 1, width, 2 * cells), bf16)]
    if with_query:
        shapes = [jax.ShapeDtypeStruct((lat * cells, width), bf16)] + shapes
    return pl.pallas_call(
        functools.partial(project_kernel, with_query, rows),
        grid=(1,),
        in_specs=[SMEM, pl.BlockSpec((lat, 1, cells, width), lambda i: (0, column, 0, 0)),
                  whole(gain), whole(weights), whole(ones)],
        out_specs=[whole(s) for s in shapes],
        out_shape=shapes,
        scratch_shapes=[pltpu.VMEM((cells, width), f32)],
        name="project",
    )(scale, tokens, gain, weights, ones)


def coarse_kernel(nblocks, scale_ref, *refs):
    blocks = refs[:nblocks]
    cin_ref, wq_ref, wk_ref, wv_ref, wo_ref, ones_ref, out_ref, coarse_ref = refs[nblocks:]
    g = pl.program_id(0)
    cell_rows, width = out_ref.shape

    @pl.when(g == 0)
    def _():
        pooled = jnp.concatenate([ref[...] for ref in blocks], axis=0)
        raw = dot((pooled / (POOL * POOL)).astype(bf16), cin_ref[...])
        coarse_ref[...] = (raw * lax.rsqrt(jnp.mean(raw * raw, axis=-1, keepdims=True) + EPS)).astype(bf16)
        out_ref[...] = jnp.zeros_like(out_ref)

    coarse = coarse_ref[...]
    sub = wq_ref.shape[1]
    heads = sub // HD
    ones = ones_ref[...]
    lane_head = lax.broadcasted_iota(jnp.int32, (cell_rows, sub), 1) // HD
    q = dot(coarse[:cell_rows], wq_ref[...])
    q = q * lax.rsqrt(block_sum(q * q, ones) + EPS) * head_scales(scale_ref, g * heads, sub)
    q = q.astype(bf16)
    k = dot(coarse, wk_ref[...])
    k = (k * lax.rsqrt(block_sum(k * k, ones) + EPS)).astype(bf16)
    v = dot(coarse, wv_ref[...]).astype(bf16)
    qbd = jnp.concatenate([jnp.where(lane_head == h, q, jnp.zeros_like(q)) for h in range(heads)], axis=0)
    s = dot(qbd, k, NT)
    e = jnp.exp(s - jnp.max(s, axis=-1, keepdims=True))
    o = dot(e.astype(bf16), v) / jnp.sum(e, axis=-1, keepdims=True)
    mixed = o[:cell_rows]
    for h in range(1, heads):
        mixed = jnp.where(lane_head == h, o[h * cell_rows:(h + 1) * cell_rows], mixed)
    out_ref[...] += dot(mixed.astype(bf16), wo_ref[...])


def coarse_level(blocks, coarse_input, coarse_project, coarse_scale, coarse_output, cell_rows, sub=256):
    width, dc = coarse_input.shape
    steps = dc // sub
    cells = sum(b.shape[0] for b in blocks)
    ones = ones_block(sub, HD)
    third = lambda t: pl.BlockSpec((dc, sub), lambda g: (0, t * steps + g))
    return pl.pallas_call(
        functools.partial(coarse_kernel, len(blocks)),
        grid=(steps,),
        in_specs=[SMEM] + [whole(b) for b in blocks]
        + [whole(coarse_input), third(0), third(1), third(2), pl.BlockSpec((sub, width), lambda g: (g, 0)), whole(ones)],
        out_specs=pl.BlockSpec((cell_rows, width), lambda g: (0, 0)),
        out_shape=jax.ShapeDtypeStruct((cell_rows, width), f32),
        scratch_shapes=[pltpu.VMEM((cells, dc), bf16)],
        name="coarse",
    )(coarse_scale, *blocks, coarse_input, coarse_project, coarse_project, coarse_project, coarse_output, ones)


def attend_kernel(rows, ncol, total_columns, near_ref, log_ref, *refs):
    q_refs = refs[:ncol]
    k_refs = refs[ncol:2 * ncol + 2]
    v_refs = refs[2 * ncol + 2:3 * ncol + 4]
    wo_ref, cu_ref, out_ref = refs[3 * ncol + 4:3 * ncol + 7]
    s_refs, m_refs, p_refs, lw_refs = (refs[3 * ncol + 7 + a * ncol:3 * ncol + 7 + (a + 1) * ncol] for a in range(4))
    i = pl.program_id(0)
    _, _, cells, width = out_ref.shape
    pairs = rows // 2
    span, reach = 4 * cells, 3 * cells

    @pl.when(i == 0)
    def _():
        for c in range(ncol):
            p_refs[c][...] = jnp.zeros_like(p_refs[c])

    first = lax.broadcasted_iota(jnp.int32, (cells, width), 1) < HD
    wo = wo_ref[...]
    zero = jnp.zeros((cells, width), bf16)

    def scores(p, c):
        off = pl.multiple_of(p * 2 * cells, 2 * cells)
        q2 = q_refs[c][pl.ds(off, 2 * cells), :]
        q0, q1 = q2[:cells], q2[cells:]
        left = jnp.concatenate([jnp.where(first, q0, zero), jnp.where(first, zero, q0), zero, zero], axis=0)
        right = jnp.concatenate([zero, zero, jnp.where(first, q1, zero), jnp.where(first, zero, q1)], axis=0)
        queries = jnp.concatenate([left, right], axis=1)
        largest = [None, None]
        for j in range(3):
            k0 = k_refs[c + j][pl.ds(off, reach), :]
            k1 = k_refs[c + j][pl.ds(pl.multiple_of(off + cells, cells), reach), :]
            s = dot(jnp.concatenate([k0, k1], axis=1), queries, NT)
            s_refs[c][j * reach:(j + 1) * reach, :] = s
            for t in range(2):
                row = i * rows + p * 2 + t
                steps = [near_ref[(row * ncol + c) * 9 + j * 3 + a] // total_columns - row for a in range(3)]
                below = sum((x < 0).astype(jnp.int32) for x in steps)
                above = sum((x > 0).astype(jnp.int32) for x in steps)
                for u, count in enumerate((below, 3 - below - above, above)):
                    log_count = log_ref[count]
                    lw_refs[c][(t * 3 + j) * 3 + u] = log_count
                    part = s[u * cells:(u + 1) * cells, t * width:(t + 1) * width]
                    part = jnp.max(part.reshape(cells // 8, 8, width), axis=0) + jnp.minimum(log_count, 0.0)
                    largest[t] = part if largest[t] is None else jnp.maximum(largest[t], part)
            if j == 2:
                for t in range(2):
                    top = jnp.max(largest[t], axis=0, keepdims=True) * LOG2E
                    m_refs[c][t * 8:(t + 1) * 8, :] = jnp.broadcast_to(top, (8, width))
            yield

    def soften(p, c):
        totals = [None, None]
        for j in range(3):
            for t in range(2):
                top = m_refs[c][t * 8:(t + 1) * 8, :]
                for u in range(3):
                    shift = top - lw_refs[c][(t * 3 + j) * 3 + u]
                    at = j * reach + u * cells
                    part = s_refs[c][at:at + cells, t * width:(t + 1) * width].reshape(cells // 8, 8, width)
                    raised = jnp.exp2(part * LOG2E - shift[None])
                    part = jnp.sum(raised, axis=0)
                    totals[t] = part if totals[t] is None else totals[t] + part
                    at = j * span + (t + u) * cells
                    p_refs[c][t, at:at + cells, :] = raised.reshape(cells, width).astype(bf16)
                if j == 2:
                    inverse = 1.0 / jnp.sum(totals[t], axis=0, keepdims=True)
                    m_refs[c][16 + t * 8:24 + t * 8, :] = jnp.broadcast_to(inverse, (8, width))
            yield

    def output(p, c):
        v = jnp.concatenate([v_refs[c + j][p + h] for j in range(3) for h in range(2)], axis=1)
        o = dot(v, jnp.concatenate([p_refs[c][0], p_refs[c][1]], axis=1))
        yield
        mixed = []
        for t in range(2):
            inverse = m_refs[c][16 + t * 8:24 + t * 8, :]
            part = o[:, t * width:(t + 1) * width].reshape(width // 8, 8, width) * inverse[None]
            part = part.reshape(width, width).T
            mixed.append(jnp.where(first, part[:cells], part[cells:]).astype(bf16))
        yield
        up = dot(jnp.concatenate(mixed, axis=0), wo)
        cu = cu_ref[pl.ds((i * rows + p * 2) // SIDE, 1), :]
        out_ref[pl.ds(p * 2, 2), c] = (up + cu).astype(bf16).reshape(2, cells, width)
        yield

    def together(*stages):
        for _ in range(3):
            for stage in stages:
                next(stage)

    together(*[scores(0, c) for c in range(ncol)])

    def body(p, carry):
        ahead, behind = jnp.minimum(p + 1, pairs - 1), jnp.maximum(p - 1, 0)
        for c in range(ncol):
            together(output(behind, c), soften(p, c), scores(ahead, c))
        return carry

    lax.fori_loop(0, pairs, body, 0)
    together(*[output(pairs - 1, c) for c in range(ncol)])


def attend(near, total_columns, qs, ks, vs, wo, cu, lat, cells, rows=16):
    ncol = len(qs)
    width = wo.shape[0]
    n = rows * cells
    logs = jnp.asarray([-1e30, 0.0, 1.0, math.log2(3.0)], f32)
    qspec = pl.BlockSpec((n, width), lambda i: (i, 0))
    kspec = pl.BlockSpec((pl.Element(n + 2 * cells), pl.Element(width)), lambda i: (i * n, 0))
    vspec = pl.BlockSpec((pl.Element(rows // 2 + 1), pl.Element(width), pl.Element(2 * cells)),
                         lambda i: (i * (rows // 2), 0, 0))
    return pl.pallas_call(
        functools.partial(attend_kernel, rows, ncol, total_columns),
        grid=(lat // rows,),
        in_specs=[SMEM, SMEM] + [qspec] * ncol + [kspec] * (ncol + 2) + [vspec] * (ncol + 2) + [whole(wo), whole(cu)],
        out_specs=pl.BlockSpec((rows, ncol, cells, width), lambda i: (i, 0, 0, 0)),
        out_shape=jax.ShapeDtypeStruct((lat, ncol, cells, width), bf16),
        scratch_shapes=[pltpu.VMEM((9 * cells, 2 * width), f32) for _ in range(ncol)]
        + [pltpu.VMEM((32, width), f32) for _ in range(ncol)]
        + [pltpu.VMEM((2, 12 * cells, width), bf16) for _ in range(ncol)]
        + [pltpu.SMEM((18,), f32) for _ in range(ncol)],
        name="attend",
    )(near, logs, *qs, *ks, *vs, wo, cu)


def shards(tokens, neighbours, time_step, time_weight, fine_project, fine_output, fine_scale,
           coarse_input, coarse_project, coarse_scale, coarse_output):
    lat, columns, cells, width = tokens.shape
    size = lax.axis_size("lon")
    up = [(i, (i + 1) % size) for i in range(size)]
    down = [(j, i) for i, j in up]
    first, last = edges(tokens)
    before = lax.ppermute(last, "lon", up)
    after = lax.ppermute(first, "lon", down)
    part, gain = pool(tokens, time_step, time_weight)
    blocks = gather_cells(part, "lon", POOL // (TILE * columns))
    ones = ones_block(width, HD)
    own = [project(tokens, c, gain, fine_project, ones, fine_scale, True) for c in range(columns)]
    cu = coarse_level(blocks, coarse_input, coarse_project, coarse_scale, coarse_output, lat // SIDE)
    sides = [project(x, 0, gain, fine_project, ones, fine_scale, False) for x in (before, after)]
    ks = [sides[0][0]] + [o[1] for o in own] + [sides[1][0]]
    vs = [sides[0][1]] + [o[2] for o in own] + [sides[1][1]]
    return attend(neighbours.reshape(-1), columns * size, [o[0] for o in own], ks, vs, fine_output, cu, lat, cells)


def solution(mesh):
    return jax.shard_map(
        shards,
        mesh=mesh,
        in_specs=(P("group", "lon", None, None), P(None, "lon", None), P("group"),
                  P(), P(), P(), P(), P(), P(), P(), P()),
        out_specs=P("group", "lon", None, None),
        check_vma=False,
    )
```
